1024 devices in a mesh: pipe: 8 (over y), dp: 8 (over z), expert: 16 (over x, core).
Axes of the slice: x: 8, y: 8, z: 8, core: 2. Of those that a mesh axis runs over, the one named last changes fastest.
Arguments:
- input_grad: bfloat16 [8, 16384, 2048], P('pipe', ('dp', 'expert')), may hold values from -0.75 to 0.75
- gate_prob: float32 [8, 16384], P('pipe', ('dp', 'expert')), may hold values from 0.2 to 1
- expert_route: int32 [8, 16384, 1], P('pipe', ('dp', 'expert')), may hold values from 0 to 7; in each aligned block of 128 rows (0 to 127, 128 to 255, ..., all dimensions but the last counted through in order) at most 32 rows name the same one
- saved_hidden: bfloat16 [8, 8, 16, 32, 22528], P('pipe', 'dp', None, None, 'expert'), may hold values from -6 to 6
Outputs:
- down_grad: bfloat16 [8, 2048, 22528], P('pipe', 'dp', 'expert')
The draws below stay inside these ranges and needn't reach their ends.
Inputs may be any that keep to these rules, and one draw needn't show every extreme that they name: `expert_route`: among the 128 tokens of one index of dp and expert no expert is named more than 32 times, and in every draw some expert is named exactly 32 times by some device's tokens.
All inputs are finite; a program needn't handle non-finite values.
Results may differ from the reference program's by a relative error of at most 0.014.
Values may be sent and summed in bfloat16 or wider, within the bound.
A program may use at most 32 MiB of HBM per device.

```python
import math
import jax
import jax.numpy as jnp
import numpy as np
from jax import lax

D = 2048
HW = 2816
SHARDS = 2
TOK = 128
EF = 8
CAP = 32
TOKENS = 16384
N_PIPE = 8
N_DP = 8
N_EXPERT = 16


def raised(values, own_key, source, target, parts, factor):
    owner, partner = [(jnp.arange(values.shape[axis_at]) // (values.shape[axis_at] // parts)).reshape([-1 if axis == axis_at else 1 for axis in range(values.ndim)]) for axis_at in (source, target)]
    chosen = jax.random.permutation(own_key, parts)[partner]
    strong = (owner == chosen) | (owner == (partner + parts // 2) % parts)
    return jnp.where(strong, factor * values, values)


def steps_of(rng, extent, cuts, low, top_value):
    level, own = 1.0, jax.random.fold_in(rng, 6)
    for dim, shards_of in cuts:
        heights = jnp.exp(jax.random.uniform(jax.random.fold_in(own, dim), (shards_of,), jnp.float32, low / len(cuts), top_value / len(cuts)))
        level = level * jnp.repeat(heights, extent[dim] // shards_of).reshape([-1 if axis == dim else 1 for axis in range(len(extent))])
    return level


def deal_out(rng, own, number, rows, amount, top, limit, slope):
    ranking = jax.random.permutation(rng, amount)
    crowded, usual = portions_of(amount, rows * top, limit, slope, True), portions_of(amount, rows * top, limit, slope, False)
    places = jnp.arange(amount)

    def named(lengths, rotation):
        used = int((lengths > 0).sum())
        fixed = max(1, used // 4)
        passed = fixed + (places - fixed + rotation * (used - fixed)) % max(1, amount - fixed)
        return jnp.zeros((amount,), jnp.int32).at[ranking[jnp.where(places < fixed, places, passed)]].set(jnp.asarray(lengths, jnp.int32))

    lengths = jnp.where(number % 4 == 0, named(crowded, number // 4), named(usual, number - number // 4 - 1))
    mixed = jax.random.permutation(jax.random.fold_in(own, 3), amount)
    source_of, receiver = mixed[0:amount // 2 * 2:2], mixed[1:amount // 2 * 2:2]
    slack = jnp.minimum(lengths[source_of] - 1, limit - lengths[receiver]) // 2
    slack = jnp.where((source_of == ranking[0]) | (receiver == ranking[0]) | (lengths[receiver] == 0), 0, jnp.maximum(slack, 0))
    passed = jax.random.randint(jax.random.fold_in(own, 4), (amount // 2,), 0, 1 << 20) % (slack + 1)
    lengths = lengths.at[source_of].add(-passed).at[receiver].add(passed)
    members = jnp.searchsorted(jnp.cumsum(lengths), jnp.arange(rows * top), side="right").astype(jnp.int32)
    grid = members.reshape(top, rows).T
    grid = grid[jax.random.permutation(jax.random.fold_in(own, 1), rows)]
    rotation = jax.random.randint(jax.random.fold_in(own, 2), (rows, 1), 0, top)
    return jnp.take_along_axis(grid, (jnp.arange(top)[None, :] + rotation) % top, axis=1)


def portions_of(count, total, most, lean, full):
    loads = [(1 << 20) // math.isqrt(grade ** lean) + 1 for grade in range(1, count + 1)]
    largest = most if full else min(most, max(-(-total // count), total * loads[0] // sum(loads)))
    least = 1 if total - largest >= count - 1 else 0
    counts, spare = [largest] + [least] * (count - 1), total - largest - least * (count - 1)
    while spare > 0:
        candidates = [i for i in range(1, count) if counts[i] < largest] or [i for i in range(1, count) if counts[i] < most]
        pool, budget = sum([loads[i] for i in candidates]), spare
        for i in candidates:
            addition = min(most - counts[i], max(1, budget * loads[i] // pool), spare)
            counts[i] = counts[i] + addition
            spare = spare - addition
    return np.array(counts)


def scatter_about(rng, dims, deviation, most, split=(), kind=jnp.bfloat16):
    drawn = deviation * jax.random.normal(rng, dims, jnp.float32)
    if split:
        drawn = drawn * steps_of(rng, dims, split, -0.22, 0.18)
    return jnp.clip(drawn, -most, most).astype(kind)


def noise_with(own_key, dims, width, bound, shards, heavy, kind=jnp.bfloat16):
    values = width * jax.random.normal(own_key, dims, jnp.float32)
    if shards:
        values = values * steps_of(own_key, dims, shards, -0.22, 0.18)
    return jnp.clip(raised(values, jax.random.fold_in(own_key, 3), *heavy), -bound, bound).astype(kind)


def setup_inputs(seed: int = 0) -> dict:
    keys = jax.random.split(jax.random.key(seed), 5)
    input_grad = noise_with(keys[0], (N_PIPE, TOKENS, D), 0.03, 0.75, ((0, 8), (1, 128)), (1, 2, 128, 5.5))
    gate_prob = jnp.clip(0.2 + 0.8 * jax.random.uniform(keys[1], (N_PIPE, TOKENS), jnp.float32) ** steps_of(keys[1], (N_PIPE, TOKENS), ((0, 8), (1, 128)), -0.2, 0.2), 0.2, 1.0)
    expert_route_keys = jax.random.split(jax.random.fold_in(keys[2], 1), N_PIPE * TOKENS // TOK)
    expert_route_turns = jax.random.permutation(jax.random.fold_in(keys[2], 3), N_PIPE * TOKENS // TOK)
    expert_route = jax.vmap(lambda own, number: deal_out(jax.random.fold_in(keys[2], 2), own, number, TOK, EF, 1, CAP, 2))(expert_route_keys, expert_route_turns).reshape((N_PIPE, TOKENS, 1))
    saved_hidden = scatter_about(keys[3], (N_PIPE, N_DP, N_EXPERT, CAP, EF * HW), 1.0, 6.0, ((0, 8), (1, 8), (4, 16)))
    return dict(input_grad=input_grad, gate_prob=gate_prob, expert_route=expert_route, saved_hidden=saved_hidden)


def slot_table(routes, flight_count, capacity):
    one_hot = (routes[..., None] == jnp.arange(flight_count, dtype=jnp.int32)).astype(jnp.int32)
    earlier = jnp.cumsum(one_hot, axis=-2) - one_hot
    position = jnp.sum(earlier * one_hot, axis=-1)
    in_slot = (position[..., None] == jnp.arange(capacity, dtype=jnp.int32)).astype(jnp.int32)
    return one_hot[..., :, None] * in_slot[..., None, :]


def reference(input_grad, gate_prob, expert_route, saved_hidden):
    flight_count = N_EXPERT // SHARDS
    grad_next = jnp.roll(input_grad, -1, axis=0)

    def one_section(pieces):
        section_grad, section_prob, section_route, section_hidden = pieces
        grad_rows = section_grad.reshape(N_DP, N_EXPERT, TOK, D)
        probs = section_prob.reshape(N_DP, N_EXPERT, TOK)
        routes = section_route[:, 0].reshape(N_DP, N_EXPERT, TOK)
        scaled = (probs[..., None] * grad_rows.astype(jnp.float32)).astype(jnp.bfloat16)
        slot_hit = slot_table(routes, flight_count, CAP).astype(jnp.float32)
        dispatched = jnp.einsum("ritec,ritd->riecd", slot_hit, scaled.astype(jnp.float32)).astype(jnp.bfloat16)
        hidden = section_hidden.reshape(N_DP, N_EXPERT, CAP, flight_count, HW)

        def one_expert(expert_index):
            rows_expert = lax.dynamic_index_in_dim(dispatched, expert_index, 2, keepdims=False)
            hidden_expert = lax.dynamic_index_in_dim(hidden, expert_index, 3, keepdims=False)
            partial_value = jnp.einsum("ricd,rich->rdh", rows_expert.astype(jnp.float32), hidden_expert.astype(jnp.float32))
            partial_value = lax.optimization_barrier(partial_value.astype(jnp.bfloat16)).astype(jnp.float32)
            return jnp.sum(partial_value, axis=0).astype(jnp.bfloat16)

        grads = lax.map(one_expert, jnp.arange(flight_count, dtype=jnp.int32))
        return jnp.transpose(grads, (1, 0, 2)).reshape(D, flight_count * HW)

    return lax.map(one_section, (grad_next, gate_prob, expert_route, saved_hidden))
```

```python
import functools

import jax
import jax.numpy as jnp
from jax import lax
from jax.experimental import pallas as pl
from jax.experimental.pallas import tpu as pltpu
from jax.sharding import PartitionSpec as P

MESH = pl.DeviceIdType.MESH


def kernel(
    sizes,
    grad_ref,
    prob_ref,
    route_ref,
    hidden_ref,
    out_ref,
    grad_in,
    outgoing,
    received,
    part,
    from_left,
    from_right,
    hidden,
    prob,
    route,
    select,
    prob_column,
    local_sems,
    grad_send,
    grad_recv,
    rows_send,
    rows_recv,
    own_sems,
    share_send,
    share_recv,
    right_send,
    right_recv,
    left_send,
    left_recv,
):
    n_pipe, n_dp, n_chip = sizes
    tokens, width = grad_ref.shape[1:]
    flights, capacity = outgoing.shape[1:3]
    blocks = n_dp
    columns = width // blocks
    half = columns // 2
    far = n_dp // 2

    section = lax.axis_index("pipe")
    replica = lax.axis_index("dp")
    index = lax.axis_index("expert")
    chip, core = index // 2, index % 2

    def along_dp(offset):
        return lax.rem(replica + offset + n_dp, n_dp)

    before = {"pipe": lax.rem(section + n_pipe - 1, n_pipe)}
    after = {"pipe": lax.rem(section + 1, n_pipe)}
    right = {"dp": along_dp(1)}
    left = {"dp": along_dp(-1)}
    sibling = {"expert": chip * 2 + 1 - core}

    def on_chip(distance):
        return lax.rem(chip + distance, n_chip)

    def peer(distance):
        return {"expert": on_chip(distance) * 2 + core}

    offsets = [far]
    for distance in range(far - 1, 0, -1):
        offsets += [distance, -distance]
    offsets.append(0)

    hidden_copy = pltpu.make_async_copy(hidden_ref.at[0, 0], hidden, local_sems.at[0])
    prob_copy = pltpu.make_async_copy(prob_ref, prob, local_sems.at[1])
    route_copy = pltpu.make_async_copy(route_ref, route, local_sems.at[2])
    hidden_copy.start()
    prob_copy.start()
    route_copy.start()

    barrier = pltpu.get_barrier_semaphore()
    partners = [before, after, right, left, sibling] + [peer(d) for d in range(1, n_chip)]
    for partner in partners:
        pl.semaphore_signal(barrier, inc=1, device_id=partner, device_id_type=MESH)
    pl.semaphore_wait(barrier, len(partners))

    def grad_copy(j):
        start = pl.multiple_of(along_dp(offsets[j]) * columns, columns)
        return pltpu.make_async_remote_copy(
            src_ref=grad_ref.at[0, :, pl.ds(start, columns)],
            dst_ref=grad_in.at[j],
            send_sem=grad_send.at[j],
            recv_sem=grad_recv.at[j],
            device_id=before,
            device_id_type=MESH,
        )

    grad_copies = [grad_copy(j) for j in range(blocks)]
    for copy in grad_copies:
        copy.start()

    prob_copy.wait()
    route_copy.wait()
    routes = route[...]
    flight_ids = lax.broadcasted_iota(jnp.int32, (flights, tokens), 0)
    one_hot = (flight_ids == routes).astype(jnp.float32)
    rows_of = lax.broadcasted_iota(jnp.int32, (tokens, tokens), 0)
    columns_of = lax.broadcasted_iota(jnp.int32, (tokens, tokens), 1)
    earlier = jnp.dot(
        one_hot.astype(jnp.bfloat16),
        (rows_of < columns_of).astype(jnp.bfloat16),
        preferred_element_type=jnp.float32,
    )
    position = jnp.sum(earlier * one_hot, axis=0, keepdims=True)
    place = routes * capacity + position.astype(jnp.int32)
    slot_ids = lax.broadcasted_iota(jnp.int32, (flights * capacity, tokens), 0)
    select[...] = (slot_ids == place).astype(jnp.float32).astype(jnp.bfloat16)
    diagonal = jnp.where(rows_of == columns_of, jnp.broadcast_to(prob[...], (tokens, tokens)), 0.0)
    prob_column[...] = jnp.broadcast_to(
        jnp.sum(diagonal, axis=1, keepdims=True), prob_column.shape
    )

    def rows_copy(j, distance):
        return pltpu.make_async_remote_copy(
            src_ref=outgoing.at[j, on_chip(distance)],
            dst_ref=received.at[j, chip, core],
            send_sem=rows_send.at[j],
            recv_sem=rows_recv.at[j],
            device_id=peer(distance),
            device_id_type=MESH,
        )

    def own_copy(j):
        return pltpu.make_async_copy(
            outgoing.at[j, chip], received.at[j, chip, core], own_sems.at[j]
        )

    def share_copy(j):
        return pltpu.make_async_remote_copy(
            src_ref=received.at[j, :, core],
            dst_ref=received.at[j, :, core],
            send_sem=share_send.at[j],
            recv_sem=share_recv.at[j],
            device_id=sibling,
            device_id_type=MESH,
        )

    def dispatch(j):
        grad_copies[j].wait_recv()
        scale = prob_column[...]
        for at in range(0, columns, scale.shape[1]):
            span = slice(at, at + scale.shape[1])
            scaled = (grad_in[j, :, span].astype(jnp.float32) * scale).astype(jnp.bfloat16)
            rows = jnp.dot(select[...], scaled, preferred_element_type=jnp.float32)
            outgoing[j, :, :, span] = rows.astype(jnp.bfloat16).reshape(
                flights, capacity, scale.shape[1]
            )
        for distance in (4, 3, 5, 2, 6, 1, 7):
            rows_copy(j, distance).start()
        own_copy(j).start()

    def share(j):
        own_copy(j).wait()
        taken = received.at[j, pl.ds(0, n_chip - 1), core]
        pltpu.make_async_copy(taken, taken, rows_recv.at[j]).wait()
        share_copy(j).start()

    def multiply(j):
        share_copy(j).wait_recv()
        rows = received[j].reshape(n_chip * 2 * capacity, columns)
        part[j] = lax.dot_general(
            rows, hidden[...], (((0,), (0,)), ((), ())), preferred_element_type=jnp.float32
        ).astype(jnp.bfloat16)

    steps = [(far, 0)]
    for distance in range(far - 1, 0, -1):
        steps += [(distance, 1), (distance, 0)]

    def chain(direction):
        to_right = direction > 0
        send, recv = (right_send, right_recv) if to_right else (left_send, left_recv)
        landing = from_left if to_right else from_right
        target = right if to_right else left
        places = []
        for distance, piece in steps:
            block = offsets.index(far if distance == far else direction * distance)
            places.append((block, piece if to_right else 1 - piece))

        def copy(n):
            block, piece = places[n]
            return pltpu.make_async_remote_copy(
                src_ref=part.at[block, pl.ds(piece * half, half)],
                dst_ref=landing.at[n],
                send_sem=send.at[n],
                recv_sem=recv.at[n],
                device_id=target,
                device_id_type=MESH,
            )

        def add(n):
            block, piece = places[n]
            span = pl.ds(piece * half, half)
            copy(n - 2).wait_recv()
            part[block, span] = (
                part[block, span].astype(jnp.float32) + landing[n - 2].astype(jnp.float32)
            ).astype(jnp.bfloat16)

        return copy, add

    right_copy, right_add = chain(1)
    left_copy, left_add = chain(-1)
    last = len(steps)

    def reduce_step(n):
        if n >= 2:
            right_add(n)
            right_copy(n).start()
            left_add(n)
            left_copy(n).start()
        else:
            right_copy(n).start()
            left_copy(n).start()

    dispatch(0)
    hidden_copy.wait()
    dispatch(1)
    dispatch(2)
    dispatch(3)
    share(0)
    dispatch(4)
    multiply(0)
    reduce_step(0)
    for j in range(5, blocks):
        dispatch(j)
    share(1)
    share(2)
    multiply(1)
    multiply(2)
    reduce_step(1)
    reduce_step(2)
    for j in range(3, blocks - 1, 2):
        share(j)
        share(j + 1)
        multiply(j)
        multiply(j + 1)
        reduce_step(j)
        reduce_step(j + 1)
    share(blocks - 1)
    multiply(blocks - 1)

    own = part.at[blocks - 1]
    pieces = [pl.ds(0, half), pl.ds(half, half)]
    right_copy(last - 2).wait_recv()
    left_copy(last - 2).wait_recv()
    for span, landing in ((pieces[1], from_left), (pieces[0], from_right)):
        own[span] = (
            own[span].astype(jnp.float32) + landing[last - 2].astype(jnp.float32)
        ).astype(jnp.bfloat16)
    right_copy(last - 1).wait_recv()
    left_copy(last - 1).wait_recv()
    for span, landing in ((pieces[0], from_left), (pieces[1], from_right)):
        out_ref[0, span] = (
            own[span].astype(jnp.float32) + landing[last - 1].astype(jnp.float32)
        ).astype(jnp.bfloat16)

    for j in range(blocks):
        grad_copies[j].wait_send()
        sent = outgoing.at[j, pl.ds(0, n_chip - 1)]
        pltpu.make_async_copy(sent, sent, rows_send.at[j]).wait()
        share_copy(j).wait_send()
    for n in range(last):
        right_copy(n).wait_send()
        left_copy(n).wait_send()


def solution(mesh):
    sizes = (mesh.shape["pipe"], mesh.shape["dp"], mesh.shape["expert"] // 2)
    n_dp, n_chip = sizes[1:]

    def body(input_grad, gate_prob, expert_route, saved_hidden):
        tokens, width = input_grad.shape[1:]
        capacity, hidden_width = saved_hidden.shape[3:]
        rows = saved_hidden.shape[2] * capacity
        columns = width // n_dp
        half = columns // 2
        chain_steps = n_dp - 1
        dma = pltpu.SemaphoreType.DMA
        anywhere = pl.BlockSpec(memory_space=pl.ANY)
        result = pl.pallas_call(
            functools.partial(kernel, sizes),
            out_shape=jax.ShapeDtypeStruct((1, columns, hidden_width), jnp.bfloat16),
            in_specs=[anywhere] * 4,
            out_specs=pl.BlockSpec(memory_space=pltpu.VMEM),
            scratch_shapes=[
                pltpu.VMEM((n_dp, tokens, columns), jnp.bfloat16),
                pltpu.VMEM((n_dp, n_chip, capacity, columns), jnp.bfloat16),
                pltpu.VMEM((n_dp, n_chip, 2, capacity, columns), jnp.bfloat16),
                pltpu.VMEM((n_dp, columns, hidden_width), jnp.bfloat16),
                pltpu.VMEM((chain_steps, half, hidden_width), jnp.bfloat16),
                pltpu.VMEM((chain_steps, half, hidden_width), jnp.bfloat16),
                pltpu.VMEM((rows, hidden_width), jnp.bfloat16),
                pltpu.VMEM((1, tokens), jnp.float32),
                pltpu.VMEM((1, tokens), jnp.int32),
                pltpu.VMEM((n_chip * capacity, tokens), jnp.bfloat16),
                pltpu.VMEM((tokens, 128), jnp.float32),
                dma((3,)),
                dma((n_dp,)),
                dma((n_dp,)),
                dma((n_dp,)),
                dma((n_dp,)),
                dma((n_dp,)),
                dma((n_dp,)),
                dma((n_dp,)),
                dma((chain_steps,)),
                dma((chain_steps,)),
                dma((chain_steps,)),
                dma((chain_steps,)),
            ],
            compiler_params=pltpu.CompilerParams(
                collective_id=0, has_side_effects=True, vmem_limit_bytes=60 * 1024 * 1024
            ),
        )(
            input_grad,
            gate_prob,
            expert_route.reshape(1, tokens),
            saved_hidden.reshape(1, 1, rows, hidden_width),
        )
        return result

    in_specs = (
        P("pipe", ("dp", "expert"), None),
        P("pipe", ("dp", "expert")),
        P("pipe", ("dp", "expert"), None),
        P("pipe", "dp", None, None, "expert"),
    )
    out_specs = P("pipe", "dp", "expert")
    return jax.shard_map(body, mesh=mesh, in_specs=in_specs, out_specs=out_specs, check_vma=False)
```

```python
import functools

import jax
import jax.numpy as jnp
from jax import lax
from jax.experimental import pallas as pl
from jax.experimental.pallas import tpu as pltpu
from jax.sharding import PartitionSpec as P

MESH = pl.DeviceIdType.MESH


def kernel(
    sizes,
    grad_ref,
    prob_ref,
    route_ref,
    hidden_ref,
    out_ref,
    grad_in,
    outgoing,
    received,
    part,
    from_left,
    from_right,
    hidden,
    prob,
    route,
    select,
    prob_column,
    local_sems,
    grad_send,
    grad_recv,
    rows_send,
    rows_recv,
    own_sems,
    share_send,
    share_recv,
    right_send,
    right_recv,
    left_send,
    left_recv,
):
    n_pipe, n_dp, n_chip = sizes
    units, tokens, columns = grad_in.shape
    flights, capacity = outgoing.shape[1:3]
    cuts = units // n_dp
    half = columns // 2
    far = n_dp // 2

    section = lax.axis_index("pipe")
    replica = lax.axis_index("dp")
    index = lax.axis_index("expert")
    chip, core = index // 2, index % 2

    def along_dp(offset):
        return lax.rem(replica + offset + n_dp, n_dp)

    before = {"pipe": lax.rem(section + n_pipe - 1, n_pipe)}
    after = {"pipe": lax.rem(section + 1, n_pipe)}
    right = {"dp": along_dp(1)}
    left = {"dp": along_dp(-1)}
    sibling = {"expert": chip * 2 + 1 - core}

    def on_chip(distance):
        return lax.rem(chip + distance, n_chip)

    def peer(distance):
        return {"expert": on_chip(distance) * 2 + core}

    order = [(far, cut) for cut in range(cuts)]
    for distance in range(far - 1, 0, -1):
        order += [(side * distance, cut) for cut in range(cuts) for side in (1, -1)]
    order += [(0, cut) for cut in range(cuts)]

    hidden_copy = pltpu.make_async_copy(hidden_ref.at[0, 0], hidden, local_sems.at[0])
    prob_copy = pltpu.make_async_copy(prob_ref, prob, local_sems.at[1])
    route_copy = pltpu.make_async_copy(route_ref, route, local_sems.at[2])
    hidden_copy.start()
    prob_copy.start()
    route_copy.start()

    barrier = pltpu.get_barrier_semaphore()
    partners = [right, left, sibling] + [peer(d) for d in range(1, n_chip)]

    for partner in partners + [after]:
        pl.semaphore_signal(barrier, inc=1, device_id=partner, device_id_type=MESH)
    pl.semaphore_wait(barrier, len(partners) + 1)

    def grad_copy(u):
        distance, cut = order[u]
        start = pl.multiple_of((along_dp(distance) * cuts + cut) * columns, columns)
        return pltpu.make_async_remote_copy(
            src_ref=grad_ref.at[0, :, pl.ds(start, columns)],
            dst_ref=grad_in.at[u],
            send_sem=grad_send.at[u],
            recv_sem=grad_recv.at[u],
            device_id=before,
            device_id_type=MESH,
        )

    for u in range(units):
        grad_copy(u).start()

    prob_copy.wait()
    route_copy.wait()
    routes = route[...]
    flight_ids = lax.broadcasted_iota(jnp.int32, (flights, tokens), 0)
    one_hot = (flight_ids == routes).astype(jnp.float32)
    rows_of = lax.broadcasted_iota(jnp.int32, (tokens, tokens), 0)
    columns_of = lax.broadcasted_iota(jnp.int32, (tokens, tokens), 1)
    earlier = jnp.dot(
        one_hot.astype(jnp.bfloat16),
        (rows_of < columns_of).astype(jnp.bfloat16),
        preferred_element_type=jnp.float32,
    )
    position = jnp.sum(earlier * one_hot, axis=0, keepdims=True)
    place = routes * capacity + position.astype(jnp.int32)
    slot_ids = lax.broadcasted_iota(jnp.int32, (flights * capacity, tokens), 0)
    select[...] = (slot_ids == place).astype(jnp.float32).astype(jnp.bfloat16)
    diagonal = jnp.where(rows_of == columns_of, jnp.broadcast_to(prob[...], (tokens, tokens)), 0.0)
    prob_column[...] = jnp.broadcast_to(
        jnp.sum(diagonal, axis=1, keepdims=True), prob_column.shape
    )

    def rows_copy(u, distance):
        return pltpu.make_async_remote_copy(
            src_ref=outgoing.at[u, on_chip(distance)],
            dst_ref=received.at[u, chip, core],
            send_sem=rows_send.at[u],
            recv_sem=rows_recv.at[u],
            device_id=peer(distance),
            device_id_type=MESH,
        )

    def own_copy(u):
        return pltpu.make_async_copy(
            outgoing.at[u, chip], received.at[u, chip, core], own_sems.at[u]
        )

    def share_copy(u):
        return pltpu.make_async_remote_copy(
            src_ref=received.at[u, :, core],
            dst_ref=received.at[u, :, core],
            send_sem=share_send.at[u],
            recv_sem=share_recv.at[u],
            device_id=sibling,
            device_id_type=MESH,
        )

    far_first = sorted(range(1, n_chip), key=lambda d: -min(d, n_chip - d))

    def dispatch(u):
        grad_copy(u).wait_recv()
        scaled = (grad_in[u].astype(jnp.float32) * prob_column[...]).astype(jnp.bfloat16)
        rows = jnp.dot(select[...], scaled, preferred_element_type=jnp.float32)
        outgoing[u] = rows.astype(jnp.bfloat16).reshape(flights, capacity, columns)
        for distance in far_first:
            rows_copy(u, distance).start()
        own_copy(u).start()

    def share(u):
        own_copy(u).wait()
        taken = received.at[u, pl.ds(0, n_chip - 1), core]
        pltpu.make_async_copy(taken, taken, rows_recv.at[u]).wait()
        share_copy(u).start()

    def multiply(u):
        share_copy(u).wait_recv()
        rows = received[u].reshape(n_chip * 2 * capacity, columns)
        part[u] = lax.dot_general(
            rows, hidden[...], (((0,), (0,)), ((), ())), preferred_element_type=jnp.float32
        ).astype(jnp.bfloat16)

    steps = [(far, cut, 0, None) for cut in range(cuts)]
    for distance in range(far - 1, 0, -1):
        for cut in range(cuts):
            for piece in (1, 0):
                source = (distance + 1, cut, piece)
                known = [step[:3] for step in steps]
                steps.append(
                    (distance, cut, piece, known.index(source) if source in known else None)
                )
    last = len(steps)

    def chain(side):
        to_right = side > 0
        send, recv = (right_send, right_recv) if to_right else (left_send, left_recv)
        landing = from_left if to_right else from_right
        target = right if to_right else left

        def place_of(n, closer=0):
            distance, cut, piece, source = steps[n]
            distance -= closer
            unit = order.index((distance if distance == far else side * distance, cut))
            row = (piece if to_right else 1 - piece) * half
            return unit, row, source

        def copy(n):
            unit, row, _ = place_of(n)
            return pltpu.make_async_remote_copy(
                src_ref=part.at[unit, pl.ds(row, half)],
                dst_ref=landing.at[n],
                send_sem=send.at[n],
                recv_sem=recv.at[n],
                device_id=target,
                device_id_type=MESH,
            )

        def advance(n):
            unit, row, source = place_of(n)
            if source is not None:
                copy(source).wait_recv()
                part[unit, pl.ds(row, half)] = (
                    part[unit, pl.ds(row, half)].astype(jnp.float32)
                    + landing[source].astype(jnp.float32)
                ).astype(jnp.bfloat16)
            copy(n).start()

        def finish(n, to_out):
            unit, row, _ = place_of(n, closer=1)
            copy(n).wait_recv()
            total = (
                part[unit, pl.ds(row, half)].astype(jnp.float32) + landing[n].astype(jnp.float32)
            ).astype(jnp.bfloat16)
            if to_out:
                out_ref[0, pl.ds(steps[n][1] * columns + row, half)] = total
            else:
                part[unit, pl.ds(row, half)] = total

        return copy, advance, finish

    right_copy, right_advance, right_finish = chain(1)
    left_copy, left_advance, left_finish = chain(-1)

    def reduce_step(n):
        right_advance(n)
        left_advance(n)

    for u in range(units // 2):
        dispatch(u)
        if u == 0:
            hidden_copy.wait()
    waiting = list(range(units // 2, units))
    done = 0
    for u in range(cuts):
        share(u)
        for later in waiting[:2]:
            dispatch(later)
        del waiting[:2]
        multiply(u)
        reduce_step(u)
        done = u + 1
    for later in waiting:
        dispatch(later)


    for u in range(cuts, units, 2):
        pair = range(u, min(u + 2, units))
        for v in pair:
            share(v)
        for v in pair:
            multiply(v)
        for n in pair:
            if n < last:
                reduce_step(n)

    for n in range(last - 2 * cuts, last):
        right_finish(n, steps[n][2] == 0)
        left_finish(n, steps[n][2] == 0)

    for u in range(units):
        grad_copy(u).wait_send()
        sent = outgoing.at[u, pl.ds(0, n_chip - 1)]
        pltpu.make_async_copy(sent, sent, rows_send.at[u]).wait()
        share_copy(u).wait_send()
    for n in range(last):
        right_copy(n).wait_send()
        left_copy(n).wait_send()


def solution(mesh):
    sizes = (mesh.shape["pipe"], mesh.shape["dp"], mesh.shape["expert"] // 2)
    n_dp, n_chip = sizes[1:]

    def body(input_grad, gate_prob, expert_route, saved_hidden):
        tokens, width = input_grad.shape[1:]
        capacity, hidden_width = saved_hidden.shape[3:]
        rows = saved_hidden.shape[2] * capacity
        columns = 128
        units = width // columns
        half = columns // 2
        chain_steps = units - units // n_dp
        dma = pltpu.SemaphoreType.DMA
        in_place = pl.BlockSpec(memory_space=pltpu.MemorySpace.HBM)
        result = pl.pallas_call(
            functools.partial(kernel, sizes),
            out_shape=jax.ShapeDtypeStruct((1, width // n_dp, hidden_width), jnp.bfloat16),
            in_specs=[in_place] * 4,
            out_specs=pl.BlockSpec(memory_space=pltpu.VMEM),
            scratch_shapes=[
                pltpu.VMEM((units, tokens, columns), jnp.bfloat16),
                pltpu.VMEM((units, n_chip, capacity, columns), jnp.bfloat16),
                pltpu.VMEM((units, n_chip, 2, capacity, columns), jnp.bfloat16),
                pltpu.VMEM((units, columns, hidden_width), jnp.bfloat16),
                pltpu.VMEM((chain_steps, half, hidden_width), jnp.bfloat16),
                pltpu.VMEM((chain_steps, half, hidden_width), jnp.bfloat16),
                pltpu.VMEM((rows, hidden_width), jnp.bfloat16),
                pltpu.VMEM((1, tokens), jnp.float32),
                pltpu.VMEM((1, tokens), jnp.int32),
                pltpu.VMEM((n_chip * capacity, tokens), jnp.bfloat16),
                pltpu.VMEM((tokens, columns), jnp.float32),
                dma((3,)),
                *[dma((units,))] * 7,
                *[dma((chain_steps,))] * 4,
            ],
            compiler_params=pltpu.CompilerParams(
                collective_id=0, has_side_effects=True, vmem_limit_bytes=24 * 1024 * 1024
            ),
        )(
            *[
                pltpu.with_memory_space_constraint(value, pltpu.MemorySpace.HBM)
                for value in (
                    input_grad,
                    gate_prob,
                    expert_route.reshape(1, tokens),
                    saved_hidden.reshape(1, 1, rows, hidden_width),
                )
            ]
        )
        return result

    in_specs = (
        P("pipe", ("dp", "expert"), None),
        P("pipe", ("dp", "expert")),
        P("pipe", ("dp", "expert"), None),
        P("pipe", "dp", None, None, "expert"),
    )
    out_specs = P("pipe", "dp", "expert")
    return jax.shard_map(body, mesh=mesh, in_specs=in_specs, out_specs=out_specs, check_vma=False)
```

```python
import functools

import jax
import jax.numpy as jnp
from jax import lax
from jax.experimental import pallas as pl
from jax.experimental.pallas import tpu as pltpu
from jax.sharding import PartitionSpec as P

MESH = pl.DeviceIdType.MESH


def kernel(
    sizes,
    grad_ref,
    prob_ref,
    route_ref,
    hidden_ref,
    out_ref,
    grad_in,
    outgoing,
    received,
    part,
    from_left,
    from_right,
    hidden,
    prob,
    route,
    select,
    prob_column,
    local_sems,
    wrap_sem,
    ahead_sems,
    behind_sems,
    grad_send,
    grad_recv,
    rows_send,
    rows_recv,
    own_sems,
    share_send,
    share_recv,
    right_send,
    right_recv,
    left_send,
    left_recv,
):
    n_pipe, n_dp, n_chip = sizes
    units, tokens, columns = grad_in.shape
    flights, capacity = outgoing.shape[1:3]
    cuts = units // n_dp
    half = columns // 2
    far = n_dp // 2

    section = lax.axis_index("pipe")
    replica = lax.axis_index("dp")
    index = lax.axis_index("expert")
    chip, core = index // 2, index % 2

    def along_dp(offset):
        return lax.rem(replica + offset + n_dp, n_dp)

    before = {"pipe": lax.rem(section + n_pipe - 1, n_pipe)}
    after = {"pipe": lax.rem(section + 1, n_pipe)}
    right = {"dp": along_dp(1)}
    left = {"dp": along_dp(-1)}
    sibling = {"expert": chip * 2 + 1 - core}

    def on_chip(distance):
        return lax.rem(chip + distance, n_chip)

    def peer(distance):
        return {"expert": on_chip(distance) * 2 + core}

    order = [(far, cut) for cut in range(cuts)]
    for distance in range(far - 1, 0, -1):
        order += [(side * distance, cut) for cut in range(cuts) for side in (1, -1)]
    order += [(0, cut) for cut in range(cuts)]

    hidden_copy = pltpu.make_async_copy(hidden_ref.at[0, 0], hidden, local_sems.at[0])
    prob_copy = pltpu.make_async_copy(prob_ref, prob, local_sems.at[1])
    route_copy = pltpu.make_async_copy(route_ref, route, local_sems.at[2])
    hidden_copy.start()
    prob_copy.start()
    route_copy.start()

    barrier = pltpu.get_barrier_semaphore()
    begins, ends = replica == 0, replica == n_dp - 1
    partners = [after, left, sibling, peer(1), peer(n_chip - 1)]
    for partner in partners:
        pl.semaphore_signal(barrier, inc=1, device_id=partner, device_id_type=MESH)

    @pl.when(jnp.logical_not(ends))
    def _():
        pl.semaphore_signal(barrier, inc=1, device_id=right, device_id_type=MESH)

    pl.semaphore_wait(barrier, len(partners) + jnp.where(begins, 0, 1))

    @pl.when(ends)
    def _():
        pl.semaphore_signal(wrap_sem, inc=1, device_id=right, device_id_type=MESH)

    def tell(sems, distance, target):
        pl.semaphore_signal(
            sems.at[distance], inc=1, device_id=target, device_id_type=MESH
        )

    tell(ahead_sems, 2, peer(n_chip - 1))
    tell(behind_sems, 2, peer(1))

    def grad_copy(u):
        distance, cut = order[u]
        start = pl.multiple_of((along_dp(distance) * cuts + cut) * columns, columns)
        return pltpu.make_async_remote_copy(
            src_ref=grad_ref.at[0, :, pl.ds(start, columns)],
            dst_ref=grad_in.at[u],
            send_sem=grad_send.at[u],
            recv_sem=grad_recv.at[u],
            device_id=before,
            device_id_type=MESH,
        )

    for u in range(units):
        grad_copy(u).start()

    prob_copy.wait()
    route_copy.wait()
    routes = route[...]
    flight_ids = lax.broadcasted_iota(jnp.int32, (flights, tokens), 0)
    one_hot = (flight_ids == routes).astype(jnp.float32)
    rows_of = lax.broadcasted_iota(jnp.int32, (tokens, tokens), 0)
    columns_of = lax.broadcasted_iota(jnp.int32, (tokens, tokens), 1)
    earlier = jnp.dot(
        one_hot.astype(jnp.bfloat16),
        (rows_of < columns_of).astype(jnp.bfloat16),
        preferred_element_type=jnp.float32,
    )
    position = jnp.sum(earlier * one_hot, axis=0, keepdims=True)
    place = routes * capacity + position.astype(jnp.int32)
    slot_ids = lax.broadcasted_iota(jnp.int32, (flights * capacity, tokens), 0)
    select[...] = (slot_ids == place).astype(jnp.float32).astype(jnp.bfloat16)
    diagonal = jnp.where(rows_of == columns_of, jnp.broadcast_to(prob[...], (tokens, tokens)), 0.0)
    prob_column[...] = jnp.broadcast_to(
        jnp.sum(diagonal, axis=1, keepdims=True), prob_column.shape
    )

    for distance in range(2, n_chip // 2 + 1):
        pl.semaphore_wait(ahead_sems.at[distance], 1)
        if distance < n_chip // 2:
            tell(ahead_sems, distance + 1, peer(n_chip - 1))
        if distance < n_chip // 2:
            pl.semaphore_wait(behind_sems.at[distance], 1)
            if distance + 1 < n_chip // 2:
                tell(behind_sems, distance + 1, peer(1))

    def rows_copy(u, distance):
        return pltpu.make_async_remote_copy(
            src_ref=outgoing.at[u, on_chip(distance)],
            dst_ref=received.at[u, chip, core],
            send_sem=rows_send.at[u],
            recv_sem=rows_recv.at[u],
            device_id=peer(distance),
            device_id_type=MESH,
        )

    def own_copy(u):
        return pltpu.make_async_copy(
            outgoing.at[u, chip], received.at[u, chip, core], own_sems.at[u]
        )

    def share_copy(u):
        return pltpu.make_async_remote_copy(
            src_ref=received.at[u, :, core],
            dst_ref=received.at[u, :, core],
            send_sem=share_send.at[u],
            recv_sem=share_recv.at[u],
            device_id=sibling,
            device_id_type=MESH,
        )

    far_first = sorted(range(1, n_chip), key=lambda d: -min(d, n_chip - d))

    def dispatch(u):
        grad_copy(u).wait_recv()
        scaled = (grad_in[u].astype(jnp.float32) * prob_column[...]).astype(jnp.bfloat16)
        rows = jnp.dot(select[...], scaled, preferred_element_type=jnp.float32)
        outgoing[u] = rows.astype(jnp.bfloat16).reshape(flights, capacity, columns)
        for distance in far_first:
            rows_copy(u, distance).start()
        own_copy(u).start()

    def share(u):
        own_copy(u).wait()
        taken = received.at[u, pl.ds(0, n_chip - 1), core]
        pltpu.make_async_copy(taken, taken, rows_recv.at[u]).wait()
        share_copy(u).start()

    def multiply(u):
        share_copy(u).wait_recv()
        rows = received[u].reshape(n_chip * 2 * capacity, columns)
        part[u] = lax.dot_general(
            rows, hidden[...], (((0,), (0,)), ((), ())), preferred_element_type=jnp.float32
        ).astype(jnp.bfloat16)

    steps = [(far, cut, 0, None) for cut in range(cuts)]
    for distance in range(far - 1, 0, -1):
        for cut in range(cuts):
            for piece in (1, 0):
                source = (distance + 1, cut, piece)
                known = [step[:3] for step in steps]
                steps.append(
                    (distance, cut, piece, known.index(source) if source in known else None)
                )
    last = len(steps)

    moved = cuts - 1

    def moved_copy():
        distance, cut, piece, _ = steps[moved]
        return pltpu.make_async_remote_copy(
            src_ref=part.at[order.index((distance, cut)), pl.ds(piece * half, half)],
            dst_ref=from_right.at[last],
            send_sem=left_send.at[last],
            recv_sem=left_recv.at[last],
            device_id=left,
            device_id_type=MESH,
        )

    def chain(side):
        to_right = side > 0
        send, recv = (right_send, right_recv) if to_right else (left_send, left_recv)
        landing = from_left if to_right else from_right
        target = right if to_right else left

        def place_of(n, closer=0):
            distance, cut, piece, source = steps[n]
            distance -= closer
            unit = order.index((distance if distance == far else side * distance, cut))
            row = (piece if to_right else 1 - piece) * half
            return unit, row, source

        def copy(n):
            unit, row, _ = place_of(min(n, last - 1))
            return pltpu.make_async_remote_copy(
                src_ref=part.at[unit, pl.ds(row, half)],
                dst_ref=landing.at[n],
                send_sem=send.at[n],
                recv_sem=recv.at[n],
                device_id=target,
                device_id_type=MESH,
            )

        def add(unit, row, slot):
            copy(slot).wait_recv()
            part[unit, pl.ds(row, half)] = (
                part[unit, pl.ds(row, half)].astype(jnp.float32)
                + landing[slot].astype(jnp.float32)
            ).astype(jnp.bfloat16)

        def advance(n):
            unit, row, source = place_of(n)
            if to_right and source == moved:
                pl.when(jnp.logical_not(begins))(lambda: add(unit, row, source))
            elif source is not None:
                add(unit, row, source)
            elif not to_right and (steps[n][0], steps[n][1], 1 - steps[n][2]) == (
                far - 1,
                steps[moved][1],
                steps[moved][2],
            ):
                pl.when(replica == n_dp - 2)(lambda: add(unit, row, last))
            if to_right and n == moved:
                pl.when(jnp.logical_not(ends))(lambda: copy(n).start())
                pl.when(ends)(lambda: moved_copy().start())
            else:
                copy(n).start()

        def finish(n, to_out):
            unit, row, _ = place_of(n, closer=1)
            copy(n).wait_recv()
            total = (
                part[unit, pl.ds(row, half)].astype(jnp.float32) + landing[n].astype(jnp.float32)
            ).astype(jnp.bfloat16)
            if to_out:
                out_ref[0, pl.ds(steps[n][1] * columns + row, half)] = total
            else:
                part[unit, pl.ds(row, half)] = total

        return copy, advance, finish

    right_copy, right_advance, right_finish = chain(1)
    left_copy, left_advance, left_finish = chain(-1)

    def reduce_step(n):
        right_advance(n)
        if n == 0:
            pl.when(begins)(lambda: pl.semaphore_wait(wrap_sem, 1))
        left_advance(n)

    for u in range(units // 2):
        dispatch(u)
        if u == 0:
            hidden_copy.wait()
    waiting = list(range(units // 2, units))
    done = 0
    for u in range(cuts):
        share(u)
        for later in waiting[:2]:
            dispatch(later)
        del waiting[:2]
        multiply(u)
        reduce_step(u)
        done = u + 1
    for later in waiting:
        dispatch(later)


    for u in range(cuts, units, 2):
        pair = range(u, min(u + 2, units))
        for v in pair:
            share(v)
        for v in pair:
            multiply(v)
        for n in pair:
            if n < last:
                reduce_step(n)

    for n in range(last - 2 * cuts, last):
        right_finish(n, steps[n][2] == 0)
        left_finish(n, steps[n][2] == 0)

    for u in range(units):
        grad_copy(u).wait_send()
        sent = outgoing.at[u, pl.ds(0, n_chip - 1)]
        pltpu.make_async_copy(sent, sent, rows_send.at[u]).wait()
        share_copy(u).wait_send()
    for n in range(last):
        if n == moved:
            pl.when(jnp.logical_not(ends))(lambda: right_copy(moved).wait_send())
            pl.when(ends)(lambda: moved_copy().wait_send())
        else:
            right_copy(n).wait_send()
        left_copy(n).wait_send()


def solution(mesh):
    sizes = (mesh.shape["pipe"], mesh.shape["dp"], mesh.shape["expert"] // 2)
    n_dp, n_chip = sizes[1:]

    def body(input_grad, gate_prob, expert_route, saved_hidden):
        tokens, width = input_grad.shape[1:]
        capacity, hidden_width = saved_hidden.shape[3:]
        rows = saved_hidden.shape[2] * capacity
        columns = 128
        units = width // columns
        half = columns // 2
        chain_steps = units - units // n_dp
        dma = pltpu.SemaphoreType.DMA
        in_place = pl.BlockSpec(memory_space=pltpu.MemorySpace.HBM)
        result = pl.pallas_call(
            functools.partial(kernel, sizes),
            out_shape=jax.ShapeDtypeStruct((1, width // n_dp, hidden_width), jnp.bfloat16),
            in_specs=[in_place] * 4,
            out_specs=pl.BlockSpec(memory_space=pltpu.VMEM),
            scratch_shapes=[
                pltpu.VMEM((units, tokens, columns), jnp.bfloat16),
                pltpu.VMEM((units, n_chip, capacity, columns), jnp.bfloat16),
                pltpu.VMEM((units, n_chip, 2, capacity, columns), jnp.bfloat16),
                pltpu.VMEM((units, columns, hidden_width), jnp.bfloat16),
                pltpu.VMEM((chain_steps, half, hidden_width), jnp.bfloat16),
                pltpu.VMEM((chain_steps + 1, half, hidden_width), jnp.bfloat16),
                pltpu.VMEM((rows, hidden_width), jnp.bfloat16),
                pltpu.VMEM((1, tokens), jnp.float32),
                pltpu.VMEM((1, tokens), jnp.int32),
                pltpu.VMEM((n_chip * capacity, tokens), jnp.bfloat16),
                pltpu.VMEM((tokens, columns), jnp.float32),
                dma((3,)),
                pltpu.SemaphoreType.REGULAR,
                pltpu.SemaphoreType.REGULAR((n_chip // 2 + 1,)),
                pltpu.SemaphoreType.REGULAR((n_chip // 2 + 1,)),
                *[dma((units,))] * 7,
                *[dma((chain_steps + 1,))] * 4,
            ],
            compiler_params=pltpu.CompilerParams(
                collective_id=0, has_side_effects=True, vmem_limit_bytes=24 * 1024 * 1024
            ),
        )(
            *[
                pltpu.with_memory_space_constraint(value, pltpu.MemorySpace.HBM)
                for value in (
                    input_grad,
                    gate_prob,
                    expert_route.reshape(1, tokens),
                    saved_hidden.reshape(1, 1, rows, hidden_width),
                )
            ]
        )
        return result

    in_specs = (
        P("pipe", ("dp", "expert"), None),
        P("pipe", ("dp", "expert")),
        P("pipe", ("dp", "expert"), None),
        P("pipe", "dp", None, None, "expert"),
    )
    out_specs = P("pipe", "dp", "expert")
    return jax.shard_map(body, mesh=mesh, in_specs=in_specs, out_specs=out_specs, check_vma=False)
```

```python
import functools

import jax
import jax.numpy as jnp
from jax import lax
from jax.experimental import pallas as pl
from jax.experimental.pallas import tpu as pltpu
from jax.sharding import PartitionSpec as P

MESH = pl.DeviceIdType.MESH


def kernel(
    sizes,
    grad_ref,
    prob_ref,
    route_ref,
    hidden_ref,
    out_ref,
    grad_in,
    outgoing,
    received,
    part,
    from_left,
    from_right,
    hidden,
    prob,
    route,
    select,
    prob_column,
    local_sems,
    wrap_sem,
    ahead_sems,
    behind_sems,
    grad_send,
    grad_recv,
    rows_send,
    rows_recv,
    own_sems,
    share_send,
    share_recv,
    right_send,
    right_recv,
    left_send,
    left_recv,
):
    n_pipe, n_dp, n_chip = sizes
    units, tokens, columns = grad_in.shape
    flights, capacity = outgoing.shape[1:3]
    cuts = units // n_dp
    half = columns // 2
    far = n_dp // 2

    section = lax.axis_index("pipe")
    replica = lax.axis_index("dp")
    index = lax.axis_index("expert")
    chip, core = index // 2, index % 2

    def along_dp(offset):
        return lax.rem(replica + offset + n_dp, n_dp)

    before = {"pipe": lax.rem(section + n_pipe - 1, n_pipe)}
    after = {"pipe": lax.rem(section + 1, n_pipe)}
    right = {"dp": along_dp(1)}
    left = {"dp": along_dp(-1)}
    sibling = {"expert": chip * 2 + 1 - core}

    def on_chip(distance):
        return lax.rem(chip + distance, n_chip)

    def peer(distance):
        return {"expert": on_chip(distance) * 2 + core}

    order = []
    for cut in range(cuts):
        order += [(far, cut), (far - 1, cut), (1 - far, cut)]
    for distance in range(far - 2, 0, -1):
        order += [(side * distance, cut) for cut in range(cuts) for side in (1, -1)]
    order += [(0, cut) for cut in range(cuts)]

    hidden_copy = pltpu.make_async_copy(hidden_ref.at[0, 0], hidden, local_sems.at[0])
    prob_copy = pltpu.make_async_copy(prob_ref, prob, local_sems.at[1])
    route_copy = pltpu.make_async_copy(route_ref, route, local_sems.at[2])
    hidden_copy.start()
    prob_copy.start()
    route_copy.start()

    barrier = pltpu.get_barrier_semaphore()
    begins, ends = replica == 0, replica == n_dp - 1
    partners = [after, left, sibling, peer(1), peer(n_chip - 1)]
    for partner in partners:
        pl.semaphore_signal(barrier, inc=1, device_id=partner, device_id_type=MESH)

    @pl.when(jnp.logical_not(ends))
    def _():
        pl.semaphore_signal(barrier, inc=1, device_id=right, device_id_type=MESH)

    pl.semaphore_wait(barrier, len(partners) + jnp.where(begins, 0, 1))

    @pl.when(ends)
    def _():
        pl.semaphore_signal(wrap_sem, inc=1, device_id=right, device_id_type=MESH)

    def tell(sems, distance, target):
        pl.semaphore_signal(
            sems.at[distance], inc=1, device_id=target, device_id_type=MESH
        )

    tell(ahead_sems, 2, peer(n_chip - 1))
    tell(behind_sems, 2, peer(1))

    def grad_copy(u):
        distance, cut = order[u]
        start = pl.multiple_of((along_dp(distance) * cuts + cut) * columns, columns)
        return pltpu.make_async_remote_copy(
            src_ref=grad_ref.at[0, :, pl.ds(start, columns)],
            dst_ref=grad_in.at[u],
            send_sem=grad_send.at[u],
            recv_sem=grad_recv.at[u],
            device_id=before,
            device_id_type=MESH,
        )

    for u in range(units):
        grad_copy(u).start()

    prob_copy.wait()
    route_copy.wait()
    routes = route[...]
    flight_ids = lax.broadcasted_iota(jnp.int32, (flights, tokens), 0)
    one_hot = (flight_ids == routes).astype(jnp.float32)
    rows_of = lax.broadcasted_iota(jnp.int32, (tokens, tokens), 0)
    columns_of = lax.broadcasted_iota(jnp.int32, (tokens, tokens), 1)
    earlier = jnp.dot(
        one_hot.astype(jnp.bfloat16),
        (rows_of < columns_of).astype(jnp.bfloat16),
        preferred_element_type=jnp.float32,
    )
    position = jnp.sum(earlier * one_hot, axis=0, keepdims=True)
    place = routes * capacity + position.astype(jnp.int32)
    slot_ids = lax.broadcasted_iota(jnp.int32, (flights * capacity, tokens), 0)
    select[...] = (slot_ids == place).astype(jnp.float32).astype(jnp.bfloat16)
    diagonal = jnp.where(rows_of == columns_of, jnp.broadcast_to(prob[...], (tokens, tokens)), 0.0)
    prob_column[...] = jnp.broadcast_to(
        jnp.sum(diagonal, axis=1, keepdims=True), prob_column.shape
    )

    for distance in range(2, n_chip // 2 + 1):
        pl.semaphore_wait(ahead_sems.at[distance], 1)
        if distance < n_chip // 2:
            tell(ahead_sems, distance + 1, peer(n_chip - 1))
        if distance < n_chip // 2:
            pl.semaphore_wait(behind_sems.at[distance], 1)
            if distance + 1 < n_chip // 2:
                tell(behind_sems, distance + 1, peer(1))

    def rows_copy(u, distance):
        return pltpu.make_async_remote_copy(
            src_ref=outgoing.at[u, on_chip(distance)],
            dst_ref=received.at[u, chip, core],
            send_sem=rows_send.at[u],
            recv_sem=rows_recv.at[u],
            device_id=peer(distance),
            device_id_type=MESH,
        )

    def own_copy(u):
        return pltpu.make_async_copy(
            outgoing.at[u, chip], received.at[u, chip, core], own_sems.at[u]
        )

    def share_copy(u):
        return pltpu.make_async_remote_copy(
            src_ref=received.at[u, :, core],
            dst_ref=received.at[u, :, core],
            send_sem=share_send.at[u],
            recv_sem=share_recv.at[u],
            device_id=sibling,
            device_id_type=MESH,
        )

    far_first = sorted(range(1, n_chip), key=lambda d: -min(d, n_chip - d))

    def dispatch(u):
        grad_copy(u).wait_recv()
        scaled = (grad_in[u].astype(jnp.float32) * prob_column[...]).astype(jnp.bfloat16)
        rows = jnp.dot(select[...], scaled, preferred_element_type=jnp.float32)
        outgoing[u] = rows.astype(jnp.bfloat16).reshape(flights, capacity, columns)
        for distance in far_first:
            rows_copy(u, distance).start()
        own_copy(u).start()

    def share(u):
        own_copy(u).wait()
        taken = received.at[u, pl.ds(0, n_chip - 1), core]
        pltpu.make_async_copy(taken, taken, rows_recv.at[u]).wait()
        share_copy(u).start()

    def multiply(u):
        share_copy(u).wait_recv()
        rows = received[u].reshape(n_chip * 2 * capacity, columns)
        part[u] = lax.dot_general(
            rows, hidden[...], (((0,), (0,)), ((), ())), preferred_element_type=jnp.float32
        ).astype(jnp.bfloat16)

    plan = [(far, 0, 0), (far - 1, 0, 1)]
    for cut in range(1, cuts):
        plan += [(far, cut, 0), (far - 1, cut - 1, 0), (far - 1, cut, 1)]
    plan.append((far - 1, cuts - 1, 0))
    for distance in range(far - 2, 0, -1):
        plan += [(distance, cut, piece) for cut in range(cuts) for piece in (1, 0)]
    steps = []
    for distance, cut, piece in plan:
        source = (distance + 1, cut, piece)
        steps.append(
            (distance, cut, piece, plan.index(source) if source in plan else None)
        )
    last = len(steps)

    moved_rows = [half * 3 // 4] + [half] * (cuts - 1)

    def moved_copy(cut):
        rows = pl.ds(0, moved_rows[cut])
        return pltpu.make_async_remote_copy(
            src_ref=part.at[order.index((far, cut)), rows],
            dst_ref=from_right.at[last + cut, rows],
            send_sem=left_send.at[last + cut],
            recv_sem=left_recv.at[last + cut],
            device_id=left,
            device_id_type=MESH,
        )

    def chain(side):
        to_right = side > 0
        send, recv = (right_send, right_recv) if to_right else (left_send, left_recv)
        landing = from_left if to_right else from_right
        target = right if to_right else left

        def place_of(n, closer=0):
            distance, cut, piece, source = steps[n]
            distance -= closer
            unit = order.index((distance if distance == far else side * distance, cut))
            row = (piece if to_right else 1 - piece) * half
            return unit, row, source

        def copy(n, offset=0, rows=half):
            unit, row, _ = place_of(min(n, last - 1))
            return pltpu.make_async_remote_copy(
                src_ref=part.at[unit, pl.ds(row + offset, rows)],
                dst_ref=landing.at[n, pl.ds(offset, rows)],
                send_sem=send.at[n],
                recv_sem=recv.at[n],
                device_id=target,
                device_id_type=MESH,
            )

        def add(unit, row, slot, offset=0, rows=half):
            copy(slot, offset, rows).wait_recv()
            span = pl.ds(row + offset, rows)
            part[unit, span] = (
                part[unit, span].astype(jnp.float32)
                + landing[slot, pl.ds(offset, rows)].astype(jnp.float32)
            ).astype(jnp.bfloat16)

        def advance(n):
            unit, row, source = place_of(n)
            distance, cut, piece, _ = steps[n]
            if to_right and source is not None and distance == far - 1:
                kept = half - moved_rows[cut]
                pl.when(jnp.logical_not(begins))(lambda: add(unit, row, source))
                if kept:
                    pl.when(begins)(lambda: add(unit, row, source, half - kept, kept))
            elif source is not None:
                add(unit, row, source)
            elif not to_right and distance == far - 1:
                pl.when(replica == n_dp - 2)(
                    lambda: add(unit, row, last + cut, 0, moved_rows[cut])
                )
            if to_right and distance == far:
                kept = half - moved_rows[cut]
                pl.when(jnp.logical_not(ends))(lambda: copy(n).start())
                if kept:
                    pl.when(ends)(lambda: copy(n, half - kept, kept).start())
                pl.when(ends)(lambda: moved_copy(cut).start())
            else:
                copy(n).start()

        def finish(n, to_out):
            unit, row, _ = place_of(n, closer=1)
            copy(n).wait_recv()
            total = (
                part[unit, pl.ds(row, half)].astype(jnp.float32) + landing[n].astype(jnp.float32)
            ).astype(jnp.bfloat16)
            if to_out:
                out_ref[0, pl.ds(steps[n][1] * columns + row, half)] = total
            else:
                part[unit, pl.ds(row, half)] = total

        return copy, advance, finish

    right_copy, right_advance, right_finish = chain(1)
    left_copy, left_advance, left_finish = chain(-1)

    ahead = list(range(units))
    to_send = {1: list(range(last)), -1: list(range(last))}

    def dispatch_next(count):
        for u in ahead[:count]:
            dispatch(u)
        del ahead[:count]

    def send_made(u):
        for n in range(u + 1):
            for side, advance in ((1, right_advance), (-1, left_advance)):
                distance = steps[n][0] if n < last else 0
                unit = (distance if distance == far else side * distance, steps[n % last][1])
                if n in to_send[side] and order.index(unit) <= u:
                    if n == 0 and side < 0:
                        pl.when(begins)(lambda: pl.semaphore_wait(wrap_sem, 1))
                    advance(n)
                    to_send[side].remove(n)

    dispatch_next(1)
    hidden_copy.wait()
    dispatch_next(3)
    for u in range(4):
        share(u)
        dispatch_next(2 if u < 2 else 1)
        multiply(u)
        send_made(u)
    for u in range(4, units, 2):
        share(u)
        share(u + 1)
        dispatch_next(2)
        multiply(u)
        send_made(u)
        multiply(u + 1)
        send_made(u + 1)

    for n in range(last - 2 * cuts, last):
        right_finish(n, steps[n][2] == 0)
        left_finish(n, steps[n][2] == 0)

    for u in range(units):
        grad_copy(u).wait_send()
        sent = outgoing.at[u, pl.ds(0, n_chip - 1)]
        pltpu.make_async_copy(sent, sent, rows_send.at[u]).wait()
        share_copy(u).wait_send()
    for n in range(last):
        distance, cut = steps[n][:2]
        if distance == far:
            kept = half - moved_rows[cut]
            pl.when(jnp.logical_not(ends))(lambda: right_copy(n).wait_send())
            if kept:
                pl.when(ends)(lambda: right_copy(n, half - kept, kept).wait_send())
            pl.when(ends)(lambda: moved_copy(cut).wait_send())
        else:
            right_copy(n).wait_send()
        left_copy(n).wait_send()


def solution(mesh):
    sizes = (mesh.shape["pipe"], mesh.shape["dp"], mesh.shape["expert"] // 2)
    n_dp, n_chip = sizes[1:]

    def body(input_grad, gate_prob, expert_route, saved_hidden):
        tokens, width = input_grad.shape[1:]
        capacity, hidden_width = saved_hidden.shape[3:]
        rows = saved_hidden.shape[2] * capacity
        columns = 128
        units = width // columns
        half = columns // 2
        chain_steps = units - units // n_dp
        dma = pltpu.SemaphoreType.DMA
        in_place = pl.BlockSpec(memory_space=pltpu.MemorySpace.HBM)
        result = pl.pallas_call(
            functools.partial(kernel, sizes),
            out_shape=jax.ShapeDtypeStruct((1, width // n_dp, hidden_width), jnp.bfloat16),
            in_specs=[in_place] * 4,
            out_specs=pl.BlockSpec(memory_space=pltpu.VMEM),
            scratch_shapes=[
                pltpu.VMEM((units, tokens, columns), jnp.bfloat16),
                pltpu.VMEM((units, n_chip, capacity, columns), jnp.bfloat16),
                pltpu.VMEM((units, n_chip, 2, capacity, columns), jnp.bfloat16),
                pltpu.VMEM((units, columns, hidden_width), jnp.bfloat16),
                pltpu.VMEM((chain_steps, half, hidden_width), jnp.bfloat16),
                pltpu.VMEM((chain_steps + units // n_dp, half, hidden_width), jnp.bfloat16),
                pltpu.VMEM((rows, hidden_width), jnp.bfloat16),
                pltpu.VMEM((1, tokens), jnp.float32),
                pltpu.VMEM((1, tokens), jnp.int32),
                pltpu.VMEM((n_chip * capacity, tokens), jnp.bfloat16),
                pltpu.VMEM((tokens, columns), jnp.float32),
                dma((3,)),
                pltpu.SemaphoreType.REGULAR,
                pltpu.SemaphoreType.REGULAR((n_chip // 2 + 1,)),
                pltpu.SemaphoreType.REGULAR((n_chip // 2 + 1,)),
                *[dma((units,))] * 7,
                *[dma((chain_steps + units // n_dp,))] * 4,
            ],
            compiler_params=pltpu.CompilerParams(
                collective_id=0, has_side_effects=True, vmem_limit_bytes=24 * 1024 * 1024
            ),
        )(
            *[
                pltpu.with_memory_space_constraint(value, pltpu.MemorySpace.HBM)
                for value in (
                    input_grad,
                    gate_prob,
                    expert_route.reshape(1, tokens),
                    saved_hidden.reshape(1, 1, rows, hidden_width),
                )
            ]
        )
        return result

    in_specs = (
        P("pipe", ("dp", "expert"), None),
        P("pipe", ("dp", "expert")),
        P("pipe", ("dp", "expert"), None),
        P("pipe", "dp", None, None, "expert"),
    )
    out_specs = P("pipe", "dp", "expert")
    return jax.shard_map(body, mesh=mesh, in_specs=in_specs, out_specs=out_specs, check_vma=False)
```

```python
import functools

import jax
import jax.numpy as jnp
from jax import lax
from jax.experimental import pallas as pl
from jax.experimental.pallas import tpu as pltpu
from jax.sharding import PartitionSpec as P

MESH = pl.DeviceIdType.MESH


def kernel(
    sizes,
    grad_ref,
    prob_ref,
    route_ref,
    hidden_ref,
    out_ref,
    grad_in,
    outgoing,
    received,
    part,
    from_left,
    from_right,
    hidden,
    prob,
    route,
    select,
    prob_column,
    local_sems,
    wrap_sem,
    ahead_sems,
    behind_sems,
    grad_send,
    grad_recv,
    rows_send,
    rows_recv,
    own_sems,
    share_send,
    share_recv,
    right_send,
    right_recv,
    left_send,
    left_recv,
):
    n_pipe, n_dp, n_chip = sizes
    units, tokens, columns = grad_in.shape
    flights, capacity = outgoing.shape[1:3]
    cuts = units // n_dp
    half = columns // 2
    far = n_dp // 2

    section = lax.axis_index("pipe")
    replica = lax.axis_index("dp")
    index = lax.axis_index("expert")
    chip, core = index // 2, index % 2

    def along_dp(offset):
        return lax.rem(replica + offset + n_dp, n_dp)

    before = {"pipe": lax.rem(section + n_pipe - 1, n_pipe)}
    after = {"pipe": lax.rem(section + 1, n_pipe)}
    right = {"dp": along_dp(1)}
    left = {"dp": along_dp(-1)}
    sibling = {"expert": chip * 2 + 1 - core}

    def on_chip(distance):
        return lax.rem(chip + distance, n_chip)

    def peer(distance):
        return {"expert": on_chip(distance) * 2 + core}

    order = []
    for cut in range(cuts):
        order += [(far, cut), (far - 1, cut), (1 - far, cut)]
    for distance in range(far - 2, 0, -1):
        order += [(side * distance, cut) for cut in range(cuts) for side in (1, -1)]
    order += [(0, cut) for cut in range(cuts)]

    hidden_copy = pltpu.make_async_copy(hidden_ref.at[0, 0], hidden, local_sems.at[0])
    prob_copy = pltpu.make_async_copy(prob_ref, prob, local_sems.at[1])
    route_copy = pltpu.make_async_copy(route_ref, route, local_sems.at[2])
    hidden_copy.start()
    prob_copy.start()
    route_copy.start()

    barrier = pltpu.get_barrier_semaphore()
    begins, ends = replica == 0, replica == n_dp - 1
    partners = [after, left, sibling, peer(1), peer(n_chip - 1)]
    for partner in partners:
        pl.semaphore_signal(barrier, inc=1, device_id=partner, device_id_type=MESH)

    @pl.when(jnp.logical_not(ends))
    def _():
        pl.semaphore_signal(barrier, inc=1, device_id=right, device_id_type=MESH)

    pl.semaphore_wait(barrier, len(partners) + jnp.where(begins, 0, 1))

    @pl.when(ends)
    def _():
        pl.semaphore_signal(wrap_sem, inc=1, device_id=right, device_id_type=MESH)

    def tell(sems, distance, target):
        pl.semaphore_signal(
            sems.at[distance], inc=1, device_id=target, device_id_type=MESH
        )

    tell(ahead_sems, 2, peer(n_chip - 1))
    tell(behind_sems, 2, peer(1))

    def grad_copy(u):
        distance, cut = order[u]
        start = pl.multiple_of((along_dp(distance) * cuts + cut) * columns, columns)
        return pltpu.make_async_remote_copy(
            src_ref=grad_ref.at[0, :, pl.ds(start, columns)],
            dst_ref=grad_in.at[u],
            send_sem=grad_send.at[u],
            recv_sem=grad_recv.at[u],
            device_id=before,
            device_id_type=MESH,
        )

    for u in range(units):
        grad_copy(u).start()

    prob_copy.wait()
    route_copy.wait()
    routes = route[...]
    flight_ids = lax.broadcasted_iota(jnp.int32, (flights, tokens), 0)
    one_hot = (flight_ids == routes).astype(jnp.float32)
    rows_of = lax.broadcasted_iota(jnp.int32, (tokens, tokens), 0)
    columns_of = lax.broadcasted_iota(jnp.int32, (tokens, tokens), 1)
    earlier = jnp.dot(
        one_hot.astype(jnp.bfloat16),
        (rows_of < columns_of).astype(jnp.bfloat16),
        preferred_element_type=jnp.float32,
    )
    position = jnp.sum(earlier * one_hot, axis=0, keepdims=True)
    place = routes * capacity + position.astype(jnp.int32)
    slot_ids = lax.broadcasted_iota(jnp.int32, (flights * capacity, tokens), 0)
    select[...] = (slot_ids == place).astype(jnp.float32).astype(jnp.bfloat16)
    diagonal = jnp.where(rows_of == columns_of, jnp.broadcast_to(prob[...], (tokens, tokens)), 0.0)
    prob_column[...] = jnp.broadcast_to(
        jnp.sum(diagonal, axis=1, keepdims=True), prob_column.shape
    )

    for distance in range(2, n_chip // 2 + 1):
        pl.semaphore_wait(ahead_sems.at[distance], 1)
        if distance < n_chip // 2:
            tell(ahead_sems, distance + 1, peer(n_chip - 1))
        if distance < n_chip // 2:
            pl.semaphore_wait(behind_sems.at[distance], 1)
            if distance + 1 < n_chip // 2:
                tell(behind_sems, distance + 1, peer(1))

    def rows_copy(u, distance):
        return pltpu.make_async_remote_copy(
            src_ref=outgoing.at[u, on_chip(distance)],
            dst_ref=received.at[u, chip, core],
            send_sem=rows_send.at[u],
            recv_sem=rows_recv.at[u],
            device_id=peer(distance),
            device_id_type=MESH,
        )

    def own_copy(u):
        return pltpu.make_async_copy(
            outgoing.at[u, chip], received.at[u, chip, core], own_sems.at[u]
        )

    def share_copy(u):
        return pltpu.make_async_remote_copy(
            src_ref=received.at[u, :, core],
            dst_ref=received.at[u, :, core],
            send_sem=share_send.at[u],
            recv_sem=share_recv.at[u],
            device_id=sibling,
            device_id_type=MESH,
        )

    far_first = sorted(range(1, n_chip), key=lambda d: -min(d, n_chip - d))

    def dispatch(u):
        grad_copy(u).wait_recv()
        scaled = (grad_in[u].astype(jnp.float32) * prob_column[...]).astype(jnp.bfloat16)
        rows = jnp.dot(select[...], scaled, preferred_element_type=jnp.float32)
        outgoing[u] = rows.astype(jnp.bfloat16).reshape(flights, capacity, columns)
        for distance in far_first:
            rows_copy(u, distance).start()
        own_copy(u).start()

    def share(u):
        own_copy(u).wait()
        taken = received.at[u, pl.ds(0, n_chip - 1), core]
        pltpu.make_async_copy(taken, taken, rows_recv.at[u]).wait()
        share_copy(u).start()

    def multiply(u):
        share_copy(u).wait_recv()
        rows = received[u].reshape(n_chip * 2 * capacity, columns)
        part[u] = lax.dot_general(
            rows, hidden[...], (((0,), (0,)), ((), ())), preferred_element_type=jnp.float32
        ).astype(jnp.bfloat16)

    plan = [(far, 0, 0), (far - 1, 0, 1)]
    for cut in range(1, cuts):
        plan += [(far, cut, 0), (far - 1, cut - 1, 0), (far - 1, cut, 1)]
    plan.append((far - 1, cuts - 1, 0))
    for distance in range(far - 2, 0, -1):
        plan += [(distance, cut, piece) for cut in range(cuts) for piece in (1, 0)]
    steps = []
    for distance, cut, piece in plan:
        source = (distance + 1, cut, piece)
        steps.append(
            (distance, cut, piece, plan.index(source) if source in plan else None)
        )
    last = len(steps)

    moved_rows = [half * 3 // 4] + [half] * (cuts - 1)

    def moved_copy(cut):
        rows = pl.ds(0, moved_rows[cut])
        return pltpu.make_async_remote_copy(
            src_ref=part.at[order.index((far, cut)), rows],
            dst_ref=from_right.at[last + cut, rows],
            send_sem=left_send.at[last + cut],
            recv_sem=left_recv.at[last + cut],
            device_id=left,
            device_id_type=MESH,
        )

    def chain(side):
        to_right = side > 0
        send, recv = (right_send, right_recv) if to_right else (left_send, left_recv)
        landing = from_left if to_right else from_right
        target = right if to_right else left

        def place_of(n, closer=0):
            distance, cut, piece, source = steps[n]
            distance -= closer
            unit = order.index((distance if distance == far else side * distance, cut))
            row = (piece if to_right else 1 - piece) * half
            return unit, row, source

        def copy(n, offset=0, rows=half):
            unit, row, _ = place_of(min(n, last - 1))
            return pltpu.make_async_remote_copy(
                src_ref=part.at[unit, pl.ds(row + offset, rows)],
                dst_ref=landing.at[n, pl.ds(offset, rows)],
                send_sem=send.at[n],
                recv_sem=recv.at[n],
                device_id=target,
                device_id_type=MESH,
            )

        def add(unit, row, slot, offset=0, rows=half):
            copy(slot, offset, rows).wait_recv()
            span = pl.ds(row + offset, rows)
            part[unit, span] = (
                part[unit, span].astype(jnp.float32)
                + landing[slot, pl.ds(offset, rows)].astype(jnp.float32)
            ).astype(jnp.bfloat16)

        def advance(n):
            unit, row, source = place_of(n)
            distance, cut, piece, _ = steps[n]
            if to_right and source is not None and distance == far - 1:
                kept = half - moved_rows[cut]
                pl.when(jnp.logical_not(begins))(lambda: add(unit, row, source))
                if kept:
                    pl.when(begins)(lambda: add(unit, row, source, half - kept, kept))
            elif source is not None:
                add(unit, row, source)
            elif not to_right and distance == far - 1:
                pl.when(replica == n_dp - 2)(
                    lambda: add(unit, row, last + cut, 0, moved_rows[cut])
                )
            if to_right and distance == far:
                kept = half - moved_rows[cut]
                pl.when(jnp.logical_not(ends))(lambda: copy(n).start())
                if kept:
                    pl.when(ends)(lambda: copy(n, half - kept, kept).start())
                pl.when(ends)(lambda: moved_copy(cut).start())
            else:
                copy(n).start()

        def finish(n, to_out):
            unit, row, _ = place_of(n, closer=1)
            copy(n).wait_recv()
            total = (
                part[unit, pl.ds(row, half)].astype(jnp.float32) + landing[n].astype(jnp.float32)
            ).astype(jnp.bfloat16)
            if to_out:
                out_ref[0, pl.ds(steps[n][1] * columns + row, half)] = total
            else:
                part[unit, pl.ds(row, half)] = total

        return copy, advance, finish

    right_copy, right_advance, right_finish = chain(1)
    left_copy, left_advance, left_finish = chain(-1)

    ahead = list(range(units))
    to_send = {1: list(range(last)), -1: list(range(last))}

    def dispatch_next(count):
        for u in ahead[:count]:
            dispatch(u)
        del ahead[:count]

    def send_made(u):
        for n in range(u + 1):
            for side, advance in ((1, right_advance), (-1, left_advance)):
                distance = steps[n][0] if n < last else 0
                unit = (distance if distance == far else side * distance, steps[n % last][1])
                if n in to_send[side] and order.index(unit) <= u:
                    if n == 0 and side < 0:
                        pl.when(begins)(lambda: pl.semaphore_wait(wrap_sem, 1))
                    advance(n)
                    to_send[side].remove(n)

    dispatch_next(1)
    hidden_copy.wait()
    dispatch_next(3)
    share(0)
    dispatch_next(1)
    for u in range(4):
        share(u + 1)
        multiply(u)
        send_made(u)
        dispatch_next(2 if u < 1 else 1)
    for u in range(4, units, 2):
        if u > 4:
            share(u)
        share(u + 1)
        dispatch_next(2)
        multiply(u)
        send_made(u)
        multiply(u + 1)
        send_made(u + 1)

    for n in range(last - 2 * cuts, last):
        right_finish(n, steps[n][2] == 0)
        left_finish(n, steps[n][2] == 0)

    for u in range(units):
        grad_copy(u).wait_send()
        sent = outgoing.at[u, pl.ds(0, n_chip - 1)]
        pltpu.make_async_copy(sent, sent, rows_send.at[u]).wait()
        share_copy(u).wait_send()
    for n in range(last):
        distance, cut = steps[n][:2]
        if distance == far:
            kept = half - moved_rows[cut]
            pl.when(jnp.logical_not(ends))(lambda: right_copy(n).wait_send())
            if kept:
                pl.when(ends)(lambda: right_copy(n, half - kept, kept).wait_send())
            pl.when(ends)(lambda: moved_copy(cut).wait_send())
        else:
            right_copy(n).wait_send()
        left_copy(n).wait_send()


def solution(mesh):
    sizes = (mesh.shape["pipe"], mesh.shape["dp"], mesh.shape["expert"] // 2)
    n_dp, n_chip = sizes[1:]

    def body(input_grad, gate_prob, expert_route, saved_hidden):
        tokens, width = input_grad.shape[1:]
        capacity, hidden_width = saved_hidden.shape[3:]
        rows = saved_hidden.shape[2] * capacity
        columns = 128
        units = width // columns
        half = columns // 2
        chain_steps = units - units // n_dp
        dma = pltpu.SemaphoreType.DMA
        in_place = pl.BlockSpec(memory_space=pltpu.MemorySpace.HBM)
        result = pl.pallas_call(
            functools.partial(kernel, sizes),
            out_shape=jax.ShapeDtypeStruct((1, width // n_dp, hidden_width), jnp.bfloat16),
            in_specs=[in_place] * 4,
            out_specs=pl.BlockSpec(memory_space=pltpu.VMEM),
            scratch_shapes=[
                pltpu.VMEM((units, tokens, columns), jnp.bfloat16),
                pltpu.VMEM((units, n_chip, capacity, columns), jnp.bfloat16),
                pltpu.VMEM((units, n_chip, 2, capacity, columns), jnp.bfloat16),
                pltpu.VMEM((units, columns, hidden_width), jnp.bfloat16),
                pltpu.VMEM((chain_steps, half, hidden_width), jnp.bfloat16),
                pltpu.VMEM((chain_steps + units // n_dp, half, hidden_width), jnp.bfloat16),
                pltpu.VMEM((rows, hidden_width), jnp.bfloat16),
                pltpu.VMEM((1, tokens), jnp.float32),
                pltpu.VMEM((1, tokens), jnp.int32),
                pltpu.VMEM((n_chip * capacity, tokens), jnp.bfloat16),
                pltpu.VMEM((tokens, columns), jnp.float32),
                dma((3,)),
                pltpu.SemaphoreType.REGULAR,
                pltpu.SemaphoreType.REGULAR((n_chip // 2 + 1,)),
                pltpu.SemaphoreType.REGULAR((n_chip // 2 + 1,)),
                *[dma((units,))] * 7,
                *[dma((chain_steps + units // n_dp,))] * 4,
            ],
            compiler_params=pltpu.CompilerParams(
                collective_id=0, has_side_effects=True, vmem_limit_bytes=24 * 1024 * 1024
            ),
        )(
            *[
                pltpu.with_memory_space_constraint(value, pltpu.MemorySpace.HBM)
                for value in (
                    input_grad,
                    gate_prob,
                    expert_route.reshape(1, tokens),
                    saved_hidden.reshape(1, 1, rows, hidden_width),
                )
            ]
        )
        return result

    in_specs = (
        P("pipe", ("dp", "expert"), None),
        P("pipe", ("dp", "expert")),
        P("pipe", ("dp", "expert"), None),
        P("pipe", "dp", None, None, "expert"),
    )
    out_specs = P("pipe", "dp", "expert")
    return jax.shard_map(body, mesh=mesh, in_specs=in_specs, out_specs=out_specs, check_vma=False)
```
